32 devices in a mesh: ctx: 16 (over z, y, x), head: 2 (over core).
Axes of the slice: x: 2, y: 2, z: 4, core: 2. Of those that a mesh axis runs over, the one named last changes fastest.
Arguments:
- queries: bfloat16 [16384, 128], P('ctx'), may hold values from -2 to 2
- keys: bfloat16 [16384, 128], P('ctx'), may hold values from -2 to 2
- values: bfloat16 [16384, 2048], P('ctx', 'head'), may hold values from -6 to 6
- gates: float32 [16, 16384], P('head', 'ctx'), may hold values from -2.5 to 0
- level_weights: float32 [16, 10, 16384], P('head', None, 'ctx'), may hold values from 0 to 4
- segment: int32 [16384], P('ctx'), may hold values from 0 to 3, never falling along the last dimension, each value on 1 to 8192 neighbouring positions
- cotangent: bfloat16 [16384, 2048], P('ctx', 'head'), may hold values from -0.59765625 to 0.59765625
Outputs:
- query_grad: float32 [16384, 128], P(('ctx', 'head'))
- key_grad: float32 [16384, 128], P(('ctx', 'head'))
- value_grad: float32 [16384, 2048], P('ctx', 'head')
- gate_grad: float32 [16, 16384], P('head', 'ctx')
- weight_grad: float32 [16, 10, 16384], P('head', None, 'ctx')
The draws below stay inside these ranges and needn't reach their ends.
Inputs may be any that keep to these rules, and one draw needn't show every extreme that they name: `segment`: document numbers never fall along the tokens; every number is used, each document holds 1 to 8192 tokens and one holds exactly that many.
All inputs are finite; a program needn't handle non-finite values.
Results may differ from the reference program's by a relative error of at most 0.0003.
Values sent between devices are 32-bit elements; how exact they have to be, the bound alone decides.
No kernel may reach another device: no remote copies, remote signals or barrier semaphores. Data moves between devices by JAX's collectives and lax.ppermute only.
A program may use at most 128 MiB of HBM per device.

```python
import math
import jax
import jax.numpy as jnp
import numpy as np
from jax import lax

HEAD_COUNT = 16
DS = 128
DV = 128
STRETCH = 128
LEVELS = 10
TOK_DEV = 1024
TOKEN_COUNT = 16384
N_CTX = 16


def draw_gates(key, part):
    random_subkeys = jax.random.split(key, 6)
    head_order = jax.random.permutation(random_subkeys[0], HEAD_COUNT)
    slow_heads = head_order < HEAD_COUNT // 2
    mixing = jax.random.uniform(random_subkeys[1], (HEAD_COUNT,), jnp.float32)
    slow_rate = jnp.exp(jnp.log(0.1 / TOKEN_COUNT) + mixing * jnp.log(6.0))
    fast_rate = jnp.exp(jnp.log(1.0 / 2000.0) + mixing * jnp.log(2000.0 / 30.0))
    baseline_rate = jnp.where(slow_heads, slow_rate, fast_rate)
    shard_scale = jnp.exp(jax.random.uniform(random_subkeys[2], (HEAD_COUNT, TOKEN_COUNT // TOK_DEV), jnp.float32, -0.7, 0.7))
    shard_scale = jnp.repeat(shard_scale, TOK_DEV, axis=1)
    entry_scale = jnp.exp(jax.random.uniform(random_subkeys[3], (HEAD_COUNT, TOKEN_COUNT), jnp.float32, -0.7, 0.7))
    spike_position = jax.random.randint(random_subkeys[4], (HEAD_COUNT, 3), 0, TOKEN_COUNT)
    spike_loss = jax.random.uniform(random_subkeys[5], (HEAD_COUNT, 3), jnp.float32, 0.2, 0.5)
    spike_hits = jnp.arange(TOKEN_COUNT)[None, None, :] == spike_position[:, :, None]
    spike_events = jnp.sum(jnp.where(spike_hits, jnp.log(1.0 - spike_loss)[:, :, None], 0.0), axis=1)
    return -(baseline_rate[:, None] * shard_scale * entry_scale) + spike_events


def draw_level_weights(key, part):
    level_idx = jnp.arange(LEVELS)
    bucket_size = jnp.where(level_idx == 0, STRETCH / 2.0, STRETCH * 2.0 ** jnp.maximum(level_idx - 1, 0))
    base_weight = bucket_size.astype(jnp.float32) ** (-0.5)
    spread = jnp.exp(jax.random.uniform(key, (HEAD_COUNT, LEVELS, TOKEN_COUNT), jnp.float32, -0.7, 0.7))
    return base_weight[None, :, None] * spread


def levels(own_key, extent, cuts, low, top_value):
    factor_of, own = 1.0, jax.random.fold_in(own_key, 6)
    for dim, blocks in cuts:
        draws = jnp.exp(jax.random.uniform(jax.random.fold_in(own, dim), (blocks,), jnp.float32, low / len(cuts), top_value / len(cuts)))
        factor_of = factor_of * jnp.repeat(draws, extent[dim] // blocks).reshape([-1 if axis == dim else 1 for axis in range(len(extent))])
    return factor_of


def profile(number_of, total, bound, lean):
    weights = [(1 << 20) // math.isqrt(rank ** lean) + 1 for rank in range(2, number_of + 1)]
    spare, holding = total - bound - (number_of - 1), [1] * (number_of - 1)
    while spare > 0:
        free = [i for i in range(number_of - 1) if holding[i] < bound]
        whole, left = sum([weights[i] for i in free]), spare
        for i in free:
            extra = min(bound - holding[i], max(1, left * weights[i] // whole), spare)
            holding[i] = holding[i] + extra
            spare = spare - extra
    return np.array([bound] + holding)


def ragged_sizes(stream_key, count, total, limit, skew):
    if count == 2:
        one = jax.random.randint(stream_key, (), max(1, total - limit), min(limit, total - 1) + 1)
        return jnp.stack([one, total - one])
    sizes = jnp.asarray(profile(count, total, limit, skew), jnp.int32)
    pairs = (count - 1) // 2
    source_of, sink = sizes[1:1 + 2 * pairs:2], sizes[2:2 + 2 * pairs:2]
    slack = jnp.minimum(source_of - 1, limit - sink)
    shifted = jax.random.randint(jax.random.fold_in(stream_key, 1), (pairs,), 0, 1 << 20) % (slack + 1)
    sizes = sizes.at[1:1 + 2 * pairs:2].set(source_of - shifted).at[2:2 + 2 * pairs:2].set(sink + shifted)
    return sizes[jax.random.permutation(jax.random.fold_in(stream_key, 2), count)]


def noise(stream_key, shape, width, bound, pieces=(), kind=jnp.bfloat16):
    loudness = levels(stream_key, shape, pieces, -0.22, 0.18) if pieces else 1.0
    result = jax.random.normal(stream_key, shape, jnp.float32) * width * loudness
    return jnp.minimum(jnp.maximum(result, -bound), bound).astype(kind)


def setup_inputs(seed: int = 0) -> dict:
    splits = jax.random.split(jax.random.key(seed), 8)
    return {
        "queries": noise(splits[0], (TOKEN_COUNT, DS), 0.3, 2.0, ((0, 16),)),
        "keys": noise(splits[1], (TOKEN_COUNT, DS), 0.3, 2.0, ((0, 16),)),
        "values": noise(splits[2], (TOKEN_COUNT, HEAD_COUNT * DV), 1.0, 6.0, ((0, 16), (1, 2))),
        "gates": draw_gates(jax.random.fold_in(splits[7], 71), 0),
        "level_weights": draw_level_weights(jax.random.fold_in(splits[7], 71), 0),
        "segment": jnp.searchsorted(jnp.cumsum(ragged_sizes(splits[5], N_CTX // 4, TOKEN_COUNT, TOKEN_COUNT // 2, 0)), jnp.arange(TOKEN_COUNT), side="right").astype(jnp.int32),
        "cotangent": noise(splits[6], (TOKEN_COUNT, HEAD_COUNT * DV), 0.09, 0.59765625, ((0, 16), (1, 2))),
    }


PRECISE = lax.Precision.HIGHEST

def stretch_tables(gates, segment):
    num_stretches = segment.shape[0] // STRETCH
    seg_stretches = segment.reshape(num_stretches, STRETCH)
    within = jnp.cumsum(gates.reshape(num_stretches, STRETCH), axis=1)
    stretch_total = within[:, -1]
    return (seg_stretches, within, stretch_total, jnp.cumsum(stretch_total), seg_stretches[:, -1])

def stretch_mix(query_stretches, key_stretches, value_stretches, seg_stretches, within, first_weight):
    offsets = jnp.arange(STRETCH)
    causal = offsets[:, None] >= offsets[None, :]
    allowed = causal[None] & (seg_stretches[:, :, None] == seg_stretches[:, None, :])
    decays = jnp.where(allowed, jnp.exp(jnp.minimum(within[:, :, None] - within[:, None, :], 0.0)), 0.0)
    scores = jnp.einsum('cti,csi->cts', query_stretches, key_stretches, precision=PRECISE)
    return jnp.einsum('cts,csj->ctj', first_weight[:, :, None] * decays * scores, value_stretches, precision=PRECISE)

def merge_blocks(blocks, block_span, stretch_cum, seg_end):
    num_blocks = blocks.shape[0]
    block_ends = jnp.arange(num_blocks) * block_span + block_span - 1
    lower_end = block_ends[0::2]
    upper_end = block_ends[1::2]
    linkage = jnp.where(seg_end[lower_end] == seg_end[upper_end], jnp.exp(jnp.minimum(stretch_cum[upper_end] - stretch_cum[lower_end], 0.0)), 0.0)
    return blocks[0::2] * linkage[:, None, None] + blocks[1::2]

def bridge(source_end, active, prior_stretch, stretch_cum, seg_end):
    source = jnp.maximum(source_end, 0)
    allowed = active & (seg_end[source] == seg_end[prior_stretch])
    return jnp.where(allowed, jnp.exp(jnp.minimum(stretch_cum[prior_stretch] - stretch_cum[source], 0.0)), 0.0)

def half_level(queries, blocks, block_span, token_weight):
    num_stretches = token_weight.shape[0]
    num_pairs = num_stretches // (2 * block_span)
    paired_weight = token_weight.reshape(num_pairs, 2, block_span * STRETCH)
    query_pairs = queries.reshape(num_pairs, 2, block_span * STRETCH, queries.shape[1])
    upper_out = jnp.einsum('nti,nij->ntj', query_pairs[:, 1] * paired_weight[:, 1, :, None], blocks[0::2], precision=PRECISE)
    return jnp.stack([jnp.zeros_like(upper_out), upper_out], axis=1).reshape(num_stretches * STRETCH, upper_out.shape[2])

def head_forward(queries, keys, values, gates, weights, segment):
    length = queries.shape[0]
    num_stretches = length // STRETCH
    seg_stretches, within, stretch_total, stretch_cum, seg_end = stretch_tables(gates, segment)
    weight_stretches = weights.reshape(LEVELS, num_stretches, STRETCH)
    key_stretches = keys.reshape(num_stretches, STRETCH, -1)
    value_stretches = values.reshape(num_stretches, STRETCH, -1)
    summed = stretch_mix(queries.reshape(num_stretches, STRETCH, -1), key_stretches, value_stretches, seg_stretches, within, weight_stretches[0]).reshape(length, -1)
    key_weight = jnp.where(seg_stretches == seg_end[:, None], jnp.exp(stretch_total[:, None] - within), 0.0)
    blocks = jnp.einsum('csi,csj->cij', key_stretches * key_weight[:, :, None], value_stretches, precision=PRECISE)
    prior_end = jnp.concatenate([jnp.full((1,), -1, jnp.int32), seg_end[:-1]])
    query_weight = jnp.where(seg_stretches == prior_end[:, None], jnp.exp(within), 0.0)
    stretch_idx = jnp.arange(num_stretches)
    prior_stretch = jnp.maximum(stretch_idx - 1, 0)
    block_span = 1
    for level_idx in range(1, LEVELS - 1):
        if 2 * block_span <= num_stretches:
            active = stretch_idx // block_span % 2 == 1
            linkage = bridge(stretch_idx // block_span * block_span - 1, active, prior_stretch, stretch_cum, seg_end)
            summed = summed + half_level(queries, blocks, block_span, linkage[:, None] * query_weight * weight_stretches[level_idx])
            blocks = merge_blocks(blocks, block_span, stretch_cum, seg_end)
            block_span = 2 * block_span
    if 2 * block_span <= num_stretches:
        num_blocks = num_stretches // block_span
        block_idx = jnp.arange(num_blocks)
        block_ends = block_idx * block_span + block_span - 1
        before_end = jnp.maximum(block_idx - 1, 0) * block_span + block_span - 1
        allowed = (block_idx[None, :] < block_idx[:, None]) & (seg_end[block_ends][None, :] == seg_end[before_end][:, None])
        prefix_mix = jnp.where(allowed, jnp.exp(jnp.minimum(stretch_cum[before_end][:, None] - stretch_cum[block_ends][None, :], 0.0)), 0.0)
        prefix = jnp.einsum('ab,bij->aij', prefix_mix, blocks, precision=PRECISE)
        linkage = bridge(stretch_idx // block_span * block_span - 1, stretch_idx >= block_span, prior_stretch, stretch_cum, seg_end)
        token_weight = (linkage[:, None] * query_weight * weight_stretches[LEVELS - 1]).reshape(num_blocks, block_span * STRETCH)
        grouped = queries.reshape(num_blocks, block_span * STRETCH, queries.shape[1]) * token_weight[:, :, None]
        summed = summed + jnp.einsum('nti,nij->ntj', grouped, prefix, precision=PRECISE).reshape(length, -1)
    return summed

def reference(queries, keys, values, gates, level_weights, segment, cotangent):
    length = queries.shape[0]
    query_full = queries.astype(jnp.float32)
    key_full = keys.astype(jnp.float32)
    value_heads = values.astype(jnp.float32).reshape(length, HEAD_COUNT, DV).transpose(1, 0, 2)
    cotan_heads = cotangent.astype(jnp.float32).reshape(length, HEAD_COUNT, DV).transpose(1, 0, 2)

    def one_head(carried, head_item):
        value_one, gate_one, weight_one, cotan_one = head_item

        def forward(query_in, key_in, value_in, gate_in, weight_in):
            return head_forward(query_in, key_in, value_in, gate_in, weight_in, segment)
        _, pullback = jax.vjp(forward, query_full, key_full, value_one, gate_one, weight_one)
        query_part, key_part, value_part, gate_part, weight_part = pullback(cotan_one)
        return ((carried[0] + query_part, carried[1] + key_part), (value_part, gate_part, weight_part))
    initial = (jnp.zeros((length, DS), jnp.float32), jnp.zeros((length, DS), jnp.float32))
    (query_grad, key_grad), (value_parts, gate_grad, weight_grad) = lax.scan(one_head, initial, (value_heads, gates, level_weights, cotan_heads))
    value_grad = value_parts.transpose(1, 0, 2).reshape(length, HEAD_COUNT * DV)
    return (query_grad, key_grad, value_grad, gate_grad, weight_grad)
```

```python
import functools

import jax
import jax.numpy as jnp
from jax import lax
from jax.experimental import pallas as pl
from jax.experimental.pallas import tpu as pltpu
from jax.sharding import PartitionSpec as P

STRETCH = 128
F32 = jnp.float32
BF16 = jnp.bfloat16


def halves(x):
    high = x.astype(BF16)
    return high, (x - high.astype(F32)).astype(BF16)


def dot_nn(a, b):
    return lax.dot_general(a, b, (((1,), (0,)), ((), ())), preferred_element_type=F32)


def dot_nt(a, b):
    return lax.dot_general(a, b, (((1,), (1,)), ((), ())), preferred_element_type=F32)


def piece(c):
    return slice(c * STRETCH, (c + 1) * STRETCH)


def within_sums(gates_ref, count):
    tiles = []
    for c in range(count):
        x = gates_ref[:, piece(c)]
        lane = lax.broadcasted_iota(jnp.int32, x.shape, 1)
        step = 1
        while step < STRETCH:
            x = x + jnp.where(lane >= step, pltpu.roll(x, step, 1), 0.0)
            step *= 2
        tiles.append(x)
    return tiles


def flip_tile(x):
    return jnp.transpose(x)


def state_kernel(bits, rows_of, q_ref, k_ref, v_ref, g_ref, gates_ref, w_ref, seg_ref, *rest):
    s_ref = rest[0]
    dr_refs = rest[1 : 1 + bits]
    kd_ref, e_ref, qt_ref, kt_ref, lhs_ref = rest[1 + bits :]
    length = q_ref.shape[0]
    count = length // STRETCH
    h = pl.program_id(0)

    @pl.when(h == 0)
    def _():
        tiles = within_sums(gates_ref, count)
        total = tiles[0][:, STRETCH - 1 :] * 0.0
        starts = []
        for c in range(count):
            starts.append(total)
            total = total + tiles[c][:, STRETCH - 1 :]
        first = seg_ref[:, 0:1]
        last = seg_ref[:, length - 1 : length]
        for c in range(count):
            run = tiles[c] + starts[c]
            seg = seg_ref[:, piece(c)]
            kd = jnp.where(seg == last, jnp.exp(total - run), 0.0)
            e = jnp.where(seg == first, jnp.exp(run), 0.0)
            for r in range(kd_ref.shape[0]):
                kd_ref[r, :, piece(c)] = kd[r : r + 1]
                e_ref[r, :, piece(c)] = e[r : r + 1]
            qt_ref[:, piece(c)] = flip_tile(q_ref[piece(c), :].astype(F32))
            kt_ref[:, piece(c)] = flip_tile(k_ref[piece(c), :].astype(F32))

    kd = kd_ref[h]
    high, low = halves(kt_ref[...] * kd)
    v = v_ref[...]
    s_ref[0] = dot_nn(high, v) + dot_nn(low, v)
    e = e_ref[h]
    size = q_ref.shape[1]
    for b in range(bits):
        high, low = halves(qt_ref[...] * (e * w_ref[0, rows_of[b] : rows_of[b] + 1, :]))
        lhs_ref[2 * b * size : (2 * b + 1) * size, :] = high
        lhs_ref[(2 * b + 1) * size : (2 * b + 2) * size, :] = low
    out = dot_nn(lhs_ref[...], g_ref[...])
    for b in range(bits):
        dr_refs[b][0] = (
            out[2 * b * size : (2 * b + 1) * size] + out[(2 * b + 1) * size : (2 * b + 2) * size]
        )


def states(q, k, v, g, gates, weights, seg, heads, bits, rows_of):
    length, size = q.shape
    width = v.shape[1] // heads
    levels = weights.shape[1]
    rows = gates.shape[0]
    full = lambda shape: pl.BlockSpec(shape, lambda h: (0,) * len(shape))
    state = jax.ShapeDtypeStruct((heads, size, width), F32)
    state_spec = pl.BlockSpec((1, size, width), lambda h: (h, 0, 0))
    return pl.pallas_call(
        functools.partial(state_kernel, bits, rows_of),
        grid=(heads,),
        in_specs=[
            full((length, size)),
            full((length, size)),
            pl.BlockSpec((length, width), lambda h: (0, h)),
            pl.BlockSpec((length, width), lambda h: (0, h)),
            full((rows, length)),
            pl.BlockSpec((1, levels, length), lambda h: (h, 0, 0)),
            full((1, length)),
        ],
        out_specs=[state_spec] * (1 + bits) + [full((heads, 1, length))] * 2,
        out_shape=[state] * (1 + bits) + [jax.ShapeDtypeStruct((heads, 1, length), F32)] * 2,
        scratch_shapes=[
            pltpu.VMEM((size, length), F32),
            pltpu.VMEM((size, length), F32),
            pltpu.VMEM((2 * bits * size, length), BF16),
        ],
        name="states",
    )(q, k, v, g, gates, weights, seg)


def factor_kernel(bits, pos_ref, table_ref, out_ref):
    shape = table_ref.shape[1:]
    count = table_ref.shape[0]
    pos = pos_ref[0]
    spread = lambda col: jnp.broadcast_to(col, shape)
    totals = [spread(table_ref[r][:, 0:1]) for r in range(count)]
    firsts = [spread(table_ref[r][:, 1:2]) for r in range(count)]
    lasts = [spread(table_ref[r][:, 2:3]) for r in range(count)]
    zero = jnp.zeros(shape, F32)

    def pick(items, low, high):
        acc = zero
        for r in range(count):
            acc = acc + jnp.where((r >= low) & (r < high), items[r], 0.0)
        return acc

    one = zero + 1.0
    for b in range(bits):
        span = 1 << b
        base = (pos >> (b + 1)) << (b + 1)
        middle = base + span
        upper = ((pos >> b) & 1) == 1
        lower_end = pick(lasts, middle - 1, middle)
        upper_end = pick(lasts, middle + span - 1, middle + span)
        through = jnp.where(lower_end == upper_end, jnp.exp(pick(totals, middle, middle + span)), 0.0)

        def lead_of(p):
            begun = pick(firsts, p, p + 1)
            return jnp.where(lower_end == begun, jnp.exp(pick(totals, middle, p)), 0.0)

        out_ref[3 * b] = jnp.where(upper, one, through)
        out_ref[3 * b + 1] = jnp.where(upper, through, one)
        out_ref[3 * b + 2] = jnp.where(upper, lead_of(pos), zero)
        if b == bits - 1:
            out_ref[3 * bits] = jnp.where(upper, zero, lead_of(pos + span))


def factors(table, position, bits):
    return pl.pallas_call(
        functools.partial(factor_kernel, bits),
        in_specs=[
            pl.BlockSpec(memory_space=pltpu.SMEM),
            pl.BlockSpec(memory_space=pltpu.VMEM),
        ],
        out_specs=pl.BlockSpec(memory_space=pltpu.VMEM),
        out_shape=jax.ShapeDtypeStruct((3 * bits + 1,) + table.shape[1:], F32),
        name="factors",
    )(position.reshape(1), table)


def local_kernel(
    heads,
    q_ref,
    k_ref,
    v_ref,
    g_ref,
    gates_ref,
    w_ref,
    seg_ref,
    segcol_ref,
    dv_ref,
    dw_ref,
    row_ref,
    dqt_ref,
    dk_ref,
    s_ref,
    b_ref,
    link_ref,
    col_ref,
    mask_ref,
    kf_ref,
    dvs_ref,
    lhs_ref,
    wit_ref,
):
    length = q_ref.shape[0]
    count = length // STRETCH
    rows = gates_ref.shape[0]
    h = pl.program_id(0)
    index = lambda c, s: c * (c + 1) // 2 + s

    @pl.when(h == 0)
    def _():
        tiles = within_sums(gates_ref, count)
        ends = [seg_ref[:, (c + 1) * STRETCH - 1 : (c + 1) * STRETCH] for c in range(count)]
        totals = [tiles[c][:, STRETCH - 1 :] for c in range(count)]
        below = lax.broadcasted_iota(jnp.int32, (STRETCH, STRETCH), 0) <= lax.broadcasted_iota(
            jnp.int32, (STRETCH, STRETCH), 1
        )
        for c in range(count):
            seg = seg_ref[:, piece(c)]
            wit_ref[c] = tiles[c]
            same = segcol_ref[piece(c), :] == seg
            mask_ref[c] = jnp.where(below & same, 0.0, -1e30)
            kf = jnp.where(seg == ends[c], jnp.exp(totals[c] - tiles[c]), 0.0)
            gap = jnp.zeros((64 - rows, STRETCH), F32)
            col_ref[piece(c), :] = flip_tile(jnp.concatenate([kf, gap, tiles[c], gap], axis=0))
            for s in range(c + 1):
                s_ref[index(c, s)] = dot_nt(k_ref[piece(s), :], q_ref[piece(c), :])
            if c > 0:
                qf = jnp.where(seg == ends[c - 1], jnp.exp(tiles[c]), 0.0)
                between = jnp.zeros_like(totals[0])
                for s in reversed(range(c)):
                    link = jnp.where(ends[s] == ends[c - 1], jnp.exp(between), 0.0)
                    link_ref[index(c, s)] = qf * link
                    between = between + totals[s]
        b_ref[...] = jnp.zeros_like(b_ref)

    shift = lax.rem(STRETCH - h, STRETCH)
    for s in range(count):
        turned = pltpu.roll(col_ref[piece(s), :], shift, 1)
        kf_ref[piece(s), :] = jnp.broadcast_to(turned[:, 0:1], (STRETCH, STRETCH))
        lag = wit_ref[s, pl.ds(h, 1), :] - turned[:, 64:65]
        dvs_ref[piece(s), :] = jnp.exp(jnp.minimum(lag, 0.0) + mask_ref[s])
    for c in range(count):
        gc = g_ref[piece(c), :]
        grads = dot_nt(v_ref[0 : (c + 1) * STRETCH, :], gc)
        sums = {}
        for s in range(c + 1):
            level = (c ^ s).bit_length()
            at = index(c, s)
            scores = s_ref[at]
            weight = w_ref[0, level : level + 1, piece(c)]
            if s < c:
                weight = weight * link_ref[at, pl.ds(h, 1), :]
                decayed = kf_ref[piece(s), :] * grads[piece(s), :]
                mixed = weight * scores
            else:
                decay = dvs_ref[piece(c), :]
                decayed = decay * grads[piece(s), :]
                mixed = weight * (decay * scores)
            part = jnp.sum(decayed * scores, axis=0, keepdims=True)
            if s < c:
                part = part * link_ref[at, pl.ds(h, 1), :]
            sums[level] = sums[level] + part if level in sums else part
            b_ref[at] = b_ref[at] + weight * decayed
            high, low = halves(mixed)
            lhs_ref[piece(s), 0:STRETCH] = high
            lhs_ref[piece(s), STRETCH:] = low
        out = dot_nn(lhs_ref[0 : (c + 1) * STRETCH, :], jnp.concatenate([gc, gc], axis=0))
        dv_ref[piece(c), :] = out[piece(c), :]
        for s in range(c):
            if s == c - 1:
                dvs_ref[piece(s), :] = out[piece(s), :]
            else:
                dvs_ref[piece(s), :] = dvs_ref[piece(s), :] + out[piece(s), :]
        rowsum = None
        for level in range(dw_ref.shape[1]):
            if level in sums:
                dw_ref[0, level : level + 1, piece(c)] = sums[level]
                term = sums[level] * w_ref[0, level : level + 1, piece(c)]
                rowsum = term if rowsum is None else rowsum + term
            else:
                dw_ref[0, level : level + 1, piece(c)] = jnp.zeros((1, STRETCH), F32)
        row_ref[0, :, piece(c)] = rowsum
    for s in range(count - 1):
        dv_ref[piece(s), :] = dv_ref[piece(s), :] + kf_ref[piece(s), :] * dvs_ref[piece(s), :]

    @pl.when(h == heads - 1)
    def _():
        dk = [None] * count
        for c in range(count):
            dq = None
            for s in range(c + 1):
                high, low = halves(b_ref[index(c, s)])
                kt = flip_tile(k_ref[piece(s), :].astype(F32)).astype(BF16)
                both = dot_nn(jnp.concatenate([kt, kt], axis=1), jnp.concatenate([high, low], axis=0))
                dq = both if dq is None else dq + both
                qc = q_ref[piece(c), :]
                both = dot_nn(jnp.concatenate([high, low], axis=1), jnp.concatenate([qc, qc], axis=0))
                if c == s:
                    dk_ref[piece(s), :] = both
                else:
                    dk_ref[piece(s), :] = dk_ref[piece(s), :] + both
            dqt_ref[:, piece(c)] = dq


def local(q, k, v, g, gates, weights, seg, segcol, heads):
    length, size = q.shape
    width = v.shape[1] // heads
    levels = weights.shape[1]
    rows = gates.shape[0]
    count = length // STRETCH
    pairs = count * (count + 1) // 2
    kept = count.bit_length()
    full = lambda shape: pl.BlockSpec(shape, lambda h: (0,) * len(shape))
    return pl.pallas_call(
        functools.partial(local_kernel, heads),
        grid=(heads,),
        in_specs=[
            full((length, size)),
            full((length, size)),
            pl.BlockSpec((length, width), lambda h: (0, h)),
            pl.BlockSpec((length, width), lambda h: (0, h)),
            full((rows, length)),
            pl.BlockSpec((1, levels, length), lambda h: (h, 0, 0)),
            full((1, length)),
            full((length, 1)),
        ],
        out_specs=[
            pl.BlockSpec((length, width), lambda h: (0, h)),
            pl.BlockSpec((1, kept, length), lambda h: (h, 0, 0)),
            pl.BlockSpec((1, 1, length), lambda h: (h, 0, 0)),
            full((size, length)),
            full((length, size)),
        ],
        out_shape=[
            jax.ShapeDtypeStruct((length, heads * width), F32),
            jax.ShapeDtypeStruct((heads, kept, length), F32),
            jax.ShapeDtypeStruct((heads, 1, length), F32),
            jax.ShapeDtypeStruct((size, length), F32),
            jax.ShapeDtypeStruct((length, size), F32),
        ],
        scratch_shapes=[
            pltpu.VMEM((pairs, STRETCH, STRETCH), F32),
            pltpu.VMEM((pairs, STRETCH, STRETCH), F32),
            pltpu.VMEM((pairs, rows, STRETCH), F32),
            pltpu.VMEM((length, STRETCH), F32),
            pltpu.VMEM((count, STRETCH, STRETCH), F32),
            pltpu.VMEM((length, STRETCH), F32),
            pltpu.VMEM((length, width), F32),
            pltpu.VMEM((length, 2 * STRETCH), BF16),
            pltpu.VMEM((count, rows, STRETCH), F32),
        ],
        cost_estimate=pl.CostEstimate(
            flops=heads * pairs * 6 * STRETCH**3,
            transcendentals=heads * length * STRETCH,
            bytes_accessed=length * heads * width * 40,
        ),
        name="local",
    )(q, k, v, g, gates, weights, seg, segcol)


def query_kernel(heads, bits, rows_of, final, parts, q_ref, g_ref, e_ref, w_ref, coef_ref, *rest):
    states_in = rest[: len(bits)]
    rest = rest[len(bits) :]
    dqt_in, row_in = rest[:2]
    dw_in = rest[2 : 2 + parts]
    dq_ref, row_ref, in_ref, dw_ref = rest[2 + parts : 6 + parts]
    qt_ref = rest[6 + parts]
    acc_ref = rest[7 + parts] if final else dq_ref
    length, size = q_ref.shape
    count = length // STRETCH
    h = pl.program_id(0)

    @pl.when(h == 0)
    def _():
        acc_ref[...] = dqt_in[...]
        in_ref[...] = jnp.zeros_like(in_ref)
        for c in range(count):
            qt_ref[:, piece(c)] = flip_tile(q_ref[piece(c), :].astype(F32))

    stacked = []
    for state in states_in:
        stacked.append(jnp.concatenate(halves(state[0]), axis=1))
    lhs = jnp.concatenate(stacked, axis=0) if len(stacked) > 1 else stacked[0]
    step = 2 * STRETCH
    total = jnp.zeros((1, step), F32)
    scale = [coef_ref[3 * b + 2, pl.ds(h, 1), 0:1] for b in bits]
    levels = dw_ref.shape[1]
    if final:
        at = 0
        for part in dw_in:
            dw_ref[0, at : at + part.shape[1], :] = part[0]
            at += part.shape[1]
        top = at + len(bits)
        if top < levels:
            dw_ref[0, top:levels, :] = jnp.zeros((levels - top, length), F32)
    else:
        at = 0
    for n in range(length // step):
        span = slice(n * step, (n + 1) * step)
        g = g_ref[span, :]
        out = dot_nt(lhs, jnp.concatenate([g, g], axis=1))
        qt = qt_ref[:, span]
        acc = acc_ref[:, span]
        rowsum = row_in[0, :, span]
        for i, b in enumerate(bits):
            block = out[i * size : (i + 1) * size]
            e = e_ref[0, :, span] * scale[i]
            w = w_ref[0, rows_of[b] : rows_of[b] + 1, span]
            grad = e * jnp.sum(qt * block, axis=0, keepdims=True)
            dw_ref[0, at + i : at + i + 1, span] = grad
            rowsum = rowsum + w * grad
            total = total + w * grad
            acc = acc + (w * e) * block
        acc_ref[:, span] = acc
        row_ref[0, :, span] = rowsum
    in_ref[pl.ds(h, 1), :] = jnp.broadcast_to(
        jnp.sum(total, axis=1, keepdims=True), (1, in_ref.shape[1])
    )

    if final:

        @pl.when(h == heads - 1)
        def _():
            for c in range(count):
                dq_ref[piece(c), :] = flip_tile(acc_ref[:, piece(c)])


def query_side(q, g, e, weights, coefs, arrived, dqt, row, dw_parts, heads, bits, rows_of, final):
    length, size = q.shape
    width = g.shape[1] // heads
    levels = weights.shape[1]
    rows = coefs.shape[1]
    by_row = pl.BlockSpec((1, 1, length), lambda h: (h, 0, 0))
    full = lambda shape: pl.BlockSpec(shape, lambda h: (0,) * len(shape))
    state_spec = pl.BlockSpec((1, size, width), lambda h: (h, 0, 0))
    kept = levels if final else len(bits)
    dq_shape = (length, size) if final else (size, length)
    return pl.pallas_call(
        functools.partial(query_kernel, heads, bits, rows_of, final, len(dw_parts)),
        grid=(heads,),
        in_specs=[
            full((length, size)),
            pl.BlockSpec((length, width), lambda h: (0, h)),
            by_row,
            pl.BlockSpec((1, levels, length), lambda h: (h, 0, 0)),
            full(coefs.shape),
        ]
        + [state_spec] * len(bits)
        + [full((size, length)), by_row]
        + [pl.BlockSpec((1, part.shape[1], length), lambda h: (h, 0, 0)) for part in dw_parts],
        out_specs=[
            full(dq_shape),
            by_row,
            full((rows, STRETCH)),
            pl.BlockSpec((1, kept, length), lambda h: (h, 0, 0)),
        ],
        out_shape=[
            jax.ShapeDtypeStruct(dq_shape, F32),
            jax.ShapeDtypeStruct((heads, 1, length), F32),
            jax.ShapeDtypeStruct((rows, STRETCH), F32),
            jax.ShapeDtypeStruct((heads, kept, length), F32),
        ],
        scratch_shapes=[pltpu.VMEM((size, length), F32)] * (2 if final else 1),
        cost_estimate=pl.CostEstimate(
            flops=heads * len(bits) * length * size * width * 4,
            transcendentals=0,
            bytes_accessed=length * heads * width * 4,
        ),
        name="query_final" if final else "query_first",
    )(q, g, e, weights, coefs, *arrived, dqt, row, *dw_parts)


def key_kernel(heads, k_ref, v_ref, d_ref, kd_ref, dvl_ref, dkl_ref, row_ref, dv_ref, dk_ref, suf_ref, col_ref, sum_ref):
    length = k_ref.shape[0]
    count = length // STRETCH
    rows = suf_ref.shape[0]
    h = pl.program_id(0)

    @pl.when(h == 0)
    def _():
        for c in range(count):
            parts = [kd_ref[r, :, piece(c)] for r in range(heads)]
            parts.append(jnp.zeros((STRETCH - heads, STRETCH), F32))
            col_ref[piece(c), :] = flip_tile(jnp.concatenate(parts, axis=0))
        dk_ref[...] = dkl_ref[...]
        sum_ref[...] = jnp.zeros_like(sum_ref)

    high, low = halves(d_ref[0])
    tall = jnp.concatenate([high, low], axis=0)
    wide = jnp.concatenate([high, low], axis=1)
    shift = lax.rem(STRETCH - h, STRETCH)
    lane = lax.broadcasted_iota(jnp.int32, (STRETCH, STRETCH), 1)
    k = k_ref[...]
    v = v_ref[...]
    for_v = dot_nn(jnp.concatenate([k, k], axis=1), tall)
    for_k = dot_nt(jnp.concatenate([v, v], axis=1), wide)
    for c in range(count):
        turned = pltpu.roll(col_ref[piece(c), :], shift, 1)
        kd = jnp.broadcast_to(turned[:, 0:1], (STRETCH, STRETCH))
        dv = dvl_ref[piece(c), :] + kd * for_v[piece(c), :]
        dv_ref[piece(c), :] = dv
        dk_ref[piece(c), :] = dk_ref[piece(c), :] + kd * for_k[piece(c), :]
        col = jnp.sum(v[piece(c), :].astype(F32) * dv, axis=1, keepdims=True)
        sum_ref[piece(c), :] = jnp.where(lane == h, col, sum_ref[piece(c), :])

    @pl.when(h == heads - 1)
    def _():
        later = None
        for c in reversed(range(count)):
            cols = flip_tile(sum_ref[piece(c), :])
            parts = [row_ref[r, :, piece(c)] for r in range(heads)]
            if rows > heads:
                parts.append(jnp.zeros((rows - heads, STRETCH), F32))
            x = jnp.concatenate(parts, axis=0) - cols[0:rows, :]
            at = lax.broadcasted_iota(jnp.int32, x.shape, 1)
            step = 1
            while step < STRETCH:
                x = x + jnp.where(at < STRETCH - step, pltpu.roll(x, STRETCH - step, 1), 0.0)
                step *= 2
            if later is not None:
                x = x + later
            suf_ref[:, piece(c)] = x
            later = x[:, 0:1]


def key_side(k, v, carried, kd, dv_local, dk_local, row, heads):
    length, size = k.shape
    width = v.shape[1] // heads
    rows = -(-heads // 8) * 8
    full = lambda shape: pl.BlockSpec(shape, lambda h: (0,) * len(shape))
    by_head = pl.BlockSpec((length, width), lambda h: (0, h))
    return pl.pallas_call(
        functools.partial(key_kernel, heads),
        grid=(heads,),
        in_specs=[
            full((length, size)),
            by_head,
            pl.BlockSpec((1, size, width), lambda h: (h, 0, 0)),
            full((heads, 1, length)),
            by_head,
            full((length, size)),
            full((heads, 1, length)),
        ],
        out_specs=[by_head, full((length, size)), full((rows, length))],
        out_shape=[
            jax.ShapeDtypeStruct((length, heads * width), F32),
            jax.ShapeDtypeStruct((length, size), F32),
            jax.ShapeDtypeStruct((rows, length), F32),
        ],
        scratch_shapes=[pltpu.VMEM((length, STRETCH), F32), pltpu.VMEM((length, STRETCH), F32)],
        cost_estimate=pl.CostEstimate(
            flops=heads * length * size * width * 8,
            transcendentals=0,
            bytes_accessed=length * heads * width * 10,
        ),
        name="keys",
    )(k, v, carried, kd, dv_local, dk_local, row)


def swapped(block, axis, bit, up=True, down=True):
    route = []
    for low in range(lax.axis_size(axis)):
        high = low | 1 << bit
        if high != low:
            route += [(low, high)] if up else []
            route += [(high, low)] if down else []
    return lax.ppermute(block, axis, route)


def scattered(x, axis):
    count = lax.axis_size(axis)
    if count != 2:
        return lax.psum_scatter(x, axis, scatter_dimension=0, tiled=True)
    part = x.shape[0] // 2
    here = lax.axis_index(axis)
    other = lax.dynamic_slice_in_dim(x, (1 - here) * part, part, 0)
    mine = lax.dynamic_slice_in_dim(x, here * part, part, 0)
    return mine + lax.ppermute(other, axis, [(0, 1), (1, 0)])


def shards(queries, keys, values, gates, level_weights, segment, cotangent):
    heads = gates.shape[0]
    length = queries.shape[0]
    levels = level_weights.shape[1]
    shard_count = lax.axis_size("ctx")
    bits = shard_count.bit_length() - 1
    position = lax.axis_index("ctx")
    inner = (length // STRETCH).bit_length()
    rows_of = [inner + b for b in range(bits)]
    assert rows_of[-1] < levels
    rows = -(-heads // 8) * 8
    gates_in = jnp.pad(gates, ((0, rows - heads), (0, 0))) if rows > heads else gates
    seg_row = segment.reshape(1, length)
    seg_col = segment.reshape(length, 1)

    lane = lax.broadcasted_iota(jnp.int32, (rows, STRETCH), 1)
    ends = segment.astype(F32)
    tile = jnp.where(
        lane == 0,
        jnp.sum(gates_in, axis=1, keepdims=True),
        jnp.where(lane == 1, ends[0], ends[length - 1]),
    )
    table = tile[None]
    for b in range(bits):
        other = swapped(table, "ctx", b)
        upper = (position >> b) & 1 == 1
        table = jnp.concatenate(
            [jnp.where(upper, other, table), jnp.where(upper, table, other)], axis=0
        )
    coefs = factors(table, position, bits)
    coef = lambda i: coefs[i, :heads, None, :]

    made = states(
        queries, keys, values, cotangent, gates_in, level_weights, seg_row, heads, bits, rows_of
    )
    state, state_grads, (kd, e) = made[0], made[1 : 1 + bits], made[1 + bits :]

    arrived = []
    held = state
    carried = None
    for i in range(bits):
        b = i
        other = swapped(held, "ctx", b, down=b < bits - 1)
        arrived.append(other)
        if b < bits - 1:
            held = coef(3 * b) * held + coef(3 * b + 1) * other
        b = bits - 1 - i
        if carried is None:
            back = swapped(state_grads[b], "ctx", b, up=False)
            carried = coef(3 * bits) * back
        else:
            sent = coef(3 * b + 1) * carried + coef(3 * b + 2) * state_grads[b]
            carried = coef(3 * b) * carried + swapped(sent, "ctx", b)

    dv_local, dw_local, row, dqt, dk_local = local(
        queries, keys, values, cotangent, gates_in, level_weights, seg_row, seg_col, heads
    )
    early = list(range(bits - 1))
    dqt, row, in_early, dw_early = query_side(
        queries, cotangent, e, level_weights, coefs, arrived[:-1], dqt, row, [], heads, early,
        rows_of, False,
    )
    dq, row, in_late, weight_grad = query_side(
        queries, cotangent, e, level_weights, coefs, arrived[-1:], dqt, row, [dw_local, dw_early],
        heads, [bits - 1], rows_of, True,
    )
    query_grad = scattered(dq, "head")
    leaving = jnp.sum(state * carried, axis=(1, 2))
    leaving = jnp.pad(leaving, (0, rows - heads)) if rows > heads else leaving
    total = in_early + in_late - leaving[:, None]
    later = jnp.zeros_like(total)
    for b in range(bits):
        other = swapped(total, "ctx", b)
        later = later + jnp.where((position >> b) & 1 == 0, other, 0.0)
        total = total + other
    value_grad, dk, suffix = key_side(keys, values, carried, kd, dv_local, dk_local, row, heads)
    key_grad = scattered(dk, "head")
    gate_grad = (suffix + later[:, 0:1])[:heads]
    return (query_grad, key_grad, value_grad, gate_grad, weight_grad)


def solution(mesh):
    return jax.shard_map(
        shards,
        mesh=mesh,
        in_specs=(
            P("ctx", None),
            P("ctx", None),
            P("ctx", "head"),
            P("head", "ctx"),
            P("head", None, "ctx"),
            P("ctx"),
            P("ctx", "head"),
        ),
        out_specs=(
            P(("ctx", "head"), None),
            P(("ctx", "head"), None),
            P("ctx", "head"),
            P("head", "ctx"),
            P("head", None, "ctx"),
        ),
        check_vma=False,
    )
```
